32 devices in a mesh: wide: 8 (over z, x), narrow: 4 (over y, core).
Axes of the slice: x: 2, y: 2, z: 4, core: 2. Of those that a mesh axis runs over, the one named last changes fastest.
Arguments:
- tokens: bfloat16 [4096, 1152], P('wide'), may hold values from -6 to 6
- cond: bfloat16 [1, 1152], replicated, may hold values from -6 to 6
- seg_ids: int32 [1, 16], replicated, may hold values from 0 to 3, never falling along the last dimension, each value on 1 to 8 neighbouring positions
- ada_weight: bfloat16 [1152, 6912], P(None, 'narrow'), may hold values from -0.1875 to 0.1875
- ada_bias: bfloat16 [6912], P('narrow'), may hold values from -3 to 3
- qkv_weight: bfloat16 [1152, 3456], P(None, 'narrow'), may hold values from -0.1875 to 0.1875
- proj_weight: bfloat16 [1152, 1152], P('narrow'), may hold values from -0.375 to 0.375
- fc1_weight: bfloat16 [1152, 4608], P(None, 'narrow'), may hold values from -0.1875 to 0.1875
- fc1_bias: bfloat16 [4608], P('narrow'), may hold values from -3 to 3
- fc2_weight: bfloat16 [4608, 1152], P('narrow'), may hold values from -0.09375 to 0.09375
- out_grad: bfloat16 [4096, 1152], P('wide'), may hold values from -6 to 6
Outputs:
- block_out: bfloat16 [4096, 1152], P('wide')
- tokens_grad: float32 [4096, 1152], P('wide')
- cond_grad: float32 [1, 1152], replicated
- ada_weight_grad: float32 [1152, 6912], P('wide', 'narrow')
- ada_bias_grad: float32 [6912], P('narrow')
- qkv_weight_grad: float32 [1152, 3456], P('wide', 'narrow')
- proj_weight_grad: float32 [1152, 1152], P('narrow', 'wide')
- fc1_weight_grad: float32 [1152, 4608], P('wide', 'narrow')
- fc1_bias_grad: float32 [4608], P('narrow')
- fc2_weight_grad: float32 [4608, 1152], P('narrow', 'wide')
The draws below stay inside these ranges and needn't reach their ends.
Inputs may be any that keep to these rules, and one draw needn't show every extreme that they name: `seg_ids`: in each sequence the clip ids never fall from frame to frame; a clip covers 1 to 8 frames, and in each sequence one clip covers exactly 8.
All inputs are finite; a program needn't handle non-finite values.
Results may differ from the reference program's by a relative error of at most 0.017.
Values may be sent and summed in bfloat16 or wider, within the bound.
A program may use at most 128 MiB of HBM per device.

```python
import math
import jax
import jax.numpy as jnp
import numpy as np
from jax import lax

D = 1152
H = 16
HD = 72
FF = 4608
F = 16
P_SIZE = 256
SEQS = 1
TOKENS = 4096


def strengthened(values, rng, source, target, blocks, factor):
    def block_of(axis_at):
        return (jnp.arange(values.shape[axis_at]) // (values.shape[axis_at] // blocks)).reshape((-1,) + (1,) * (values.ndim - 1 - axis_at))

    one_side = jax.random.permutation(rng, blocks)[block_of(target)]
    far = (block_of(target) + blocks // 2) % blocks
    return jnp.where((block_of(source) == one_side) | (block_of(source) == far), factor * values, values)


def block_levels(stream_key, shape, shards, low, high):
    level = 1.0
    for position, parts in shards:
        draws = jax.random.uniform(jax.random.fold_in(jax.random.fold_in(stream_key, 6), position), (parts,), jnp.float32, low / len(shards), high / len(shards))
        level = level * jnp.repeat(jnp.exp(draws), shape[position] // parts).reshape((-1,) + (1,) * (len(shape) - 1 - position))
    return level


def length_profile(number_of, total, limit, slope):
    portions = [(1 << 20) // math.isqrt(grade ** slope) + 1 for grade in range(2, number_of + 1)]
    spare, counts = total - limit - (number_of - 1), [1] * (number_of - 1)
    while spare > 0:
        free = [i for i in range(number_of - 1) if counts[i] < limit]
        whole, remaining = sum([portions[i] for i in free]), spare
        for i in free:
            more = min(limit - counts[i], max(1, remaining * portions[i] // whole), spare)
            counts[i] = counts[i] + more
            spare = spare - more
    return np.array([limit] + counts)


def uneven_parts(own_key, number_of, total, reach, slope):
    if number_of == 2:
        one = jax.random.randint(own_key, (), max(1, total - reach), min(reach, total - 1) + 1)
        return jnp.stack([one, total - one])
    lengths = jnp.asarray(length_profile(number_of, total, reach, slope), jnp.int32)
    couples = (number_of - 1) // 2
    giver, receiver = lengths[1:1 + 2 * couples:2], lengths[2:2 + 2 * couples:2]
    margin = jnp.minimum(giver - 1, reach - receiver)
    moved = jax.random.randint(jax.random.fold_in(own_key, 1), (couples,), 0, 1 << 20) % (margin + 1)
    lengths = lengths.at[1:1 + 2 * couples:2].set(giver - moved).at[2:2 + 2 * couples:2].set(receiver + moved)
    return lengths[jax.random.permutation(jax.random.fold_in(own_key, 2), number_of)]


def scatter_about(stream_key, dims, deviation, limit, cuts=(), kind=jnp.bfloat16):
    result = jax.random.normal(stream_key, dims, jnp.float32) * deviation
    if len(cuts) > 0:
        result = block_levels(stream_key, dims, cuts, -0.22, 0.18) * result
    return jnp.clip(result, min=-limit, max=limit).astype(kind)


def gaussian_with(stream_key, extent, spread, bound, cuts, heavy, kind=jnp.bfloat16):
    values = spread * jax.random.normal(stream_key, extent, jnp.float32)
    if cuts:
        values = values * block_levels(stream_key, extent, cuts, -0.22, 0.18)
    return jnp.clip(strengthened(values, jax.random.fold_in(stream_key, 3), *heavy), -bound, bound).astype(kind)


def setup_inputs(seed: int = 0) -> dict:
    arg_keys = jax.random.split(jax.random.key(seed), 12)
    tokens = gaussian_with(arg_keys[0], (TOKENS, D), 1.0, 6.0, ((0, 8),), (0, 1, 8, 2.0))
    cond = scatter_about(arg_keys[1], (SEQS, D), 1.0, 6.0)
    seg_ids = jax.vmap(lambda own: jnp.searchsorted(jnp.cumsum(uneven_parts(own, 4, F, 8, 1)), jnp.arange(F), side="right"))(jax.random.split(arg_keys[2], SEQS)).reshape((SEQS, F)).astype(jnp.int32)
    ada_weight = scatter_about(arg_keys[3], (D, 6 * D), D ** -0.5, 0.1875, ((1, 4),))
    ada_bias = scatter_about(arg_keys[4], (6 * D,), 0.5, 3.0, ((0, 4),))
    qkv_weight = scatter_about(arg_keys[5], (D, 3 * D), D ** -0.5, 0.1875, ((1, 4),))
    proj_weight = scatter_about(arg_keys[6], (D, D), (D // 4) ** -0.5, 0.375, ((0, 4),))
    fc1_weight = scatter_about(arg_keys[7], (D, FF), D ** -0.5, 0.1875, ((1, 4),))
    fc1_bias = scatter_about(arg_keys[8], (FF,), 0.5, 3.0, ((0, 4),))
    fc2_weight = scatter_about(arg_keys[9], (FF, D), FF ** -0.5, 0.09375, ((0, 4),))
    out_grad = gaussian_with(arg_keys[10], (TOKENS, D), 1.0, 6.0, ((0, 8),), (0, 1, 8, 2.0))
    return {"tokens": tokens, "cond": cond, "seg_ids": seg_ids, "ada_weight": ada_weight, "ada_bias": ada_bias, "qkv_weight": qkv_weight, "proj_weight": proj_weight, "fc1_weight": fc1_weight, "fc1_bias": fc1_bias, "fc2_weight": fc2_weight, "out_grad": out_grad}


@jax.custom_vjp
def low(v):
    return lax.optimization_barrier(v.astype(jnp.bfloat16)).astype(jnp.float32)

@jax.custom_vjp
def low_back(v):
    return v

def low_keep(v):
    return (low(v), None)

def low_pass(kept, grad):
    return (grad,)

def back_keep(v):
    return (v, None)

def back_low(kept, grad):
    return (low(grad),)
low.defvjp(low_keep, low_pass)
low_back.defvjp(back_keep, back_low)
EPSILON = 1e-06
MASKED = -1e+30

def matmul_high(left, right):
    return jnp.dot(left, right, precision=lax.Precision.HIGHEST, preferred_element_type=jnp.float32)

def layer_norm(values):
    row_mean = lax.optimization_barrier(jnp.mean(values, axis=-1, keepdims=True))
    centred = values - row_mean
    row_var = lax.optimization_barrier(jnp.mean(centred * centred, axis=-1, keepdims=True))
    return centred * lax.rsqrt(row_var + EPSILON)

def modulate(values, shift, scale):
    return layer_norm(values) * (1.0 + scale) + shift

def sequence_block(tokens_seq, mods_seq, clip_ids, qkv_weight, proj_weight, fc1_weight, fc1_bias, fc2_weight):
    shift_one, scale_one, gate_one, shift_two, scale_two, gate_two = jnp.split(mods_seq, 6)
    normed_one = low(modulate(tokens_seq, shift_one, scale_one))
    qkv_all = low_back(low(matmul_high(normed_one, qkv_weight))).reshape(P_SIZE, F, H, 3, HD)
    queries = qkv_all[:, :, :, 0]
    key_rows = qkv_all[:, :, :, 1]
    value_rows = qkv_all[:, :, :, 2]
    scale_factor = 1.0 / math.sqrt(HD)
    scores = low_back(jnp.einsum('pfhd,pghd->phfg', queries, key_rows, precision=lax.Precision.HIGHEST, preferred_element_type=jnp.float32) * scale_factor)
    allowed = clip_ids[:, None] == clip_ids[None, :]
    probs = low(jax.nn.softmax(jnp.where(allowed, scores, MASKED), axis=-1))
    heads_out = jnp.einsum('phfg,pghd->pfhd', probs, value_rows, precision=lax.Precision.HIGHEST, preferred_element_type=jnp.float32)
    heads_out = low_back(low(heads_out)).reshape(P_SIZE * F, D)
    attention = low_back(matmul_high(heads_out, proj_weight))
    middle = tokens_seq + gate_one * attention
    normed_two = low(modulate(middle, shift_two, scale_two))
    pre_act = low_back(matmul_high(normed_two, fc1_weight) + fc1_bias)
    activated = low(jax.nn.gelu(pre_act, approximate=True))
    mlp_out = low_back(matmul_high(activated, fc2_weight))
    return middle + gate_two * mlp_out

def block_forward(tokens_f, cond_f, ada_weight, ada_bias, qkv_weight, proj_weight, fc1_weight, fc1_bias, fc2_weight, seg_ids):
    mods = low_back(matmul_high(low(jax.nn.silu(cond_f)), ada_weight) + ada_bias)
    seq_count = cond_f.shape[0]
    grouped = tokens_f.reshape(seq_count, P_SIZE * F, D)

    def one_sequence(member):
        return sequence_block(member[0], member[1], member[2], qkv_weight, proj_weight, fc1_weight, fc1_bias, fc2_weight)
    results = lax.map(jax.checkpoint(one_sequence), (grouped, mods, seg_ids))
    return results.reshape(seq_count * P_SIZE * F, D)

def reference(tokens, cond, seg_ids, ada_weight, ada_bias, qkv_weight, proj_weight, fc1_weight, fc1_bias, fc2_weight, out_grad):
    floats = [member.astype(jnp.float32) for member in (tokens, cond, ada_weight, ada_bias, qkv_weight, proj_weight, fc1_weight, fc1_bias, fc2_weight)]

    def forward_all(tokens_f, cond_f, ada_weight_f, ada_bias_f, qkv_weight_f, proj_weight_f, fc1_weight_f, fc1_bias_f, fc2_weight_f):
        return block_forward(tokens_f, cond_f, ada_weight_f, ada_bias_f, qkv_weight_f, proj_weight_f, fc1_weight_f, fc1_bias_f, fc2_weight_f, seg_ids)
    block_out, pullback = jax.vjp(forward_all, *floats)
    grads = pullback(out_grad.astype(jnp.float32))
    return (block_out.astype(jnp.bfloat16), grads[0], grads[1], grads[2], grads[3], grads[4], grads[5], grads[6], grads[7], grads[8])
```

```python
import functools
import math

import jax
import jax.numpy as jnp
from jax import lax
from jax.experimental import pallas as pl
from jax.experimental.pallas import tpu as pltpu
from jax.sharding import PartitionSpec as P

HD = 72
F = 16
P_SIZE = 256
EPSILON = 1e-06
MASKED = -1e30
MESH = pl.DeviceIdType.MESH
BF = jnp.bfloat16
F32 = jnp.float32
TILE = 128
CHUNK = 32
COLS = 384


def dot_nn(left, right):
    return lax.dot_general(left, right, (((1,), (0,)), ((), ())), preferred_element_type=F32)


def dot_nt(left, right):
    return lax.dot_general(left, right, (((1,), (1,)), ((), ())), preferred_element_type=F32)


def dot_tn(left, right):
    return lax.dot_general(left, right, (((0,), (0,)), ((), ())), preferred_element_type=F32)


def normalise(values):
    centred = values - jnp.mean(values, axis=-1, keepdims=True)
    scale = lax.rsqrt(jnp.mean(centred * centred, axis=-1, keepdims=True) + EPSILON)
    return centred * scale, scale


def norm_pull(normed, inverse, scaled):
    mean_a = jnp.mean(scaled, axis=-1, keepdims=True)
    mean_an = jnp.mean(scaled * normed, axis=-1, keepdims=True)
    return inverse * (scaled - mean_a - normed * mean_an)


def part(index, size):
    return pl.ds(pl.multiple_of(index * size, size), size)


class Names:
    pass


def block_kernel(names, dims, *refs):
    m = Names()
    for name, ref in zip(names, refs):
        setattr(m, name, ref)
    seqs, share, width, heads = dims
    rows = 4 * share
    group = 2 * share
    wide = lax.axis_index("wide")
    narrow = lax.axis_index("narrow")
    y, c = narrow // 2, narrow % 2
    seq = wide * rows // (P_SIZE * F)
    partner = (wide, y * 2 + 1 - c)
    across = (wide, (1 - y) * 2 + c)
    corner = (wide, (1 - y) * 2 + 1 - c)
    mine = 2 * c + y
    mine_y = 2 * c + 1 - y
    mine_p = 2 * (1 - c) + y
    mine_py = 2 * (1 - c) + 1 - y

    def remote(src, dst, index, device):
        return pltpu.make_async_remote_copy(
            src_ref=src,
            dst_ref=dst,
            send_sem=m.sent.at[index],
            recv_sem=m.got.at[index],
            device_id=device,
            device_id_type=MESH,
        )

    def load(src, dst, index):
        copy = pltpu.make_async_copy(src, dst, m.loaded.at[index])
        copy.start()
        return copy

    barrier = pltpu.get_barrier_semaphore()
    peers = (partner, across, corner)
    for peer in peers:
        pl.semaphore_signal(barrier, inc=1, device_id=peer, device_id_type=MESH)
    get_ada = load(m.ada_h, m.ada, 0)
    get_tok = load(m.tok_h, m.tok, 1)
    get_qkvw = load(m.qkvw_h, m.qkvw, 2)
    get_og = load(m.og_h, m.og, 3)
    get_projw = load(m.projw_h, m.projw, 4)
    get_w2 = load(m.w2_h, m.w2, 5)
    get_w1 = load(m.w1_h, m.w1, 6)

    cond = m.cond[...].astype(F32)
    low = cond * jax.nn.sigmoid(cond)
    if seqs == 1:
        low = jnp.broadcast_to(low, (16, width))
    else:
        low = jnp.concatenate([low] * (16 // seqs), axis=0)
    get_ada.wait()
    local = dot_nn(low.astype(BF), m.ada[...])[0:seqs] + m.adab[...].astype(F32)
    m.mods_all[narrow] = local
    pl.semaphore_wait(barrier, len(peers))
    sends = []
    for index, peer in enumerate(peers):
        sends.append(remote(m.mods_all.at[narrow], m.mods_all.at[narrow], index, peer))
        sends[-1].start()
    for index, peer in enumerate(peers):
        remote(m.mods_all.at[peer[1]], m.mods_all.at[peer[1]], index, peer).wait_recv()
    half = width // 2
    for piece in range(12):
        lanes = pl.ds((piece % 3) * half, half)
        m.mods[piece // 2 : piece // 2 + 1, (piece % 2) * half : (piece % 2 + 1) * half] = (
            m.mods_all[piece // 3, pl.ds(seq, 1), (piece % 3) * half : (piece % 3 + 1) * half]
        )

    def mod(index):
        return m.mods[index : index + 1, :]

    get_tok.wait()

    @pl.loop(0, rows // CHUNK)
    def _(step):
        at = part(step, CHUNK)
        normed, _ = normalise(m.tok[at, :].astype(F32))
        m.nrm1[at, :] = (normed * (1.0 + mod(1)) + mod(0)).astype(BF)

    get_qkvw.wait()

    @pl.loop(0, 2)
    def _(step):
        at = part(step, group)
        m.qkv[at, :] = dot_nn(m.nrm1[at, :], m.qkvw[...]).astype(BF)

    def clip_of(axis):
        frame = lax.broadcasted_iota(jnp.int32, (TILE, TILE), axis) % F
        clip = jnp.zeros((TILE, TILE), jnp.int32)
        for spot in range(F):
            clip = jnp.where(frame == spot, m.seg[seq, spot], clip)
        return clip + 8 * (lax.broadcasted_iota(jnp.int32, (TILE, TILE), axis) // F)

    allowed = clip_of(0) == clip_of(1)
    m.bias[...] = jnp.where(allowed, 0.0, MASKED)
    factor = 1.0 / math.sqrt(HD)

    def head(base, which):
        start = base * 3 * HD + which * HD
        return slice(start, start + HD)

    @pl.loop(0, rows // TILE)
    def _(step):
        at = part(step, TILE)
        for h in range(heads):
            scores = dot_nt(m.qkv[at, head(h, 0)], m.qkv[at, head(h, 1)]) * factor
            scores = jnp.where(m.bias[...] < 0.0, MASKED, scores)
            weights = jnp.exp(scores - jnp.max(scores, axis=-1, keepdims=True))
            probs = weights / jnp.sum(weights, axis=-1, keepdims=True)
            m.probs[step * heads + h] = probs
            out = dot_nn(probs.astype(BF), m.qkv[at, head(h, 2)])
            m.heads[at, h * HD : (h + 1) * HD] = out.astype(BF)

    def scatter(fill, own, other, first, second, relay, index):
        fill(1 - c, other, BF)
        one = remote(other.at[part(1 - y, share), :], first.at[0], index, partner)
        two = remote(other.at[part(y, share), :], first.at[1], index + 1, partner)
        one.start()
        two.start()
        fill(c, own, F32)
        one.wait_recv()
        relay[...] = (own[part(1 - y, share), :] + first[0].astype(F32)).astype(BF)
        three = remote(relay, second, index + 2, across)
        three.start()

        def finish():
            two.wait_recv()
            three.wait_recv()

        def value(at_row):
            kept = own[pl.ds(pl.multiple_of(y * share + at_row, CHUNK), CHUNK), :]
            here = pl.ds(pl.multiple_of(at_row, CHUNK), CHUNK)
            return kept + first[1, here, :].astype(F32) + second[here, :].astype(F32)

        def drain():
            one.wait_send()
            two.wait_send()
            three.wait_send()

        return finish, value, drain

    def gather(buffer, index):
        def at(block):
            return buffer.at[part(block, share), :]

        one = remote(at(mine), at(mine), index, across)
        two = remote(at(mine), at(mine), index + 1, partner)
        one.start()
        two.start()

        def relay():
            remote(at(mine_y), at(mine_y), index, across).wait_recv()
            three = remote(at(mine_y), at(mine_y), index + 2, partner)
            three.start()
            remote(at(mine_p), at(mine_p), index + 1, partner).wait_recv()
            return three

        def finish(three):
            remote(at(mine_py), at(mine_py), index + 2, partner).wait_recv()

        def drain(three):
            one.wait_send()
            two.wait_send()
            three.wait_send()

        return relay, finish, drain

    def mine_rows(at_row):
        return pl.ds(pl.multiple_of(mine * share + at_row, CHUNK), CHUNK)

    def over_share(body):
        @pl.loop(0, share // CHUNK)
        def _(step):
            at_row = step * CHUNK
            body(at_row, pl.ds(pl.multiple_of(at_row, CHUNK), CHUNK), mine_rows(at_row))

    def add_sum(index, values):
        m.sums[index : index + 1, :] += jnp.sum(values, axis=0, keepdims=True)

    m.sums[...] = jnp.zeros_like(m.sums)
    m.bias_sum[...] = jnp.zeros_like(m.bias_sum)

    def fill_proj(which, out, kind):
        @pl.loop(0, width // COLS)
        def _(step):
            lanes = part(step, COLS)
            out[:, lanes] = dot_nn(m.heads[part(which, group), :], m.projw[:, lanes]).astype(kind)

    get_projw.wait()
    finish, att_value, att_drain = scatter(
        fill_proj, m.own, m.other, m.first0, m.second0, m.relay, 3
    )
    get_og.wait()

    @pl.loop(0, rows // CHUNK)
    def _(step):
        at = part(step, CHUNK)
        m.mlpg[at, :] = (mod(5) * m.og[at, :].astype(F32)).astype(BF)

    finish()

    def second_norm(at_row, here, there):
        att = att_value(at_row)
        m.att[here, :] = att
        middle = m.tok[there, :].astype(F32) + mod(2) * att
        m.middle[here, :] = middle
        normed, _ = normalise(middle)
        m.nrm2[there, :] = (normed * (1.0 + mod(4)) + mod(3)).astype(BF)

    over_share(second_norm)
    att_drain()
    relay, finish, nrm2_drain = gather(m.nrm2, 6)

    get_w2.wait()

    def hidden_grad(which):
        @pl.loop(0, m.w2.shape[0] // COLS)
        def _(step):
            lanes = part(step, COLS)
            at = part(which, group)
            m.agrad[at, lanes] = dot_nt(m.mlpg[at, :], m.w2[lanes, :])

    hidden_grad(0)
    three = relay()
    hidden_grad(1)
    get_w1.wait()
    finish(three)
    root = math.sqrt(2.0 / math.pi)

    @pl.loop(0, 2 * (m.w1.shape[1] // COLS))
    def _(step):
        at = part(step % 2, group)
        lanes = part(step // 2, COLS)
        pre = dot_nn(m.nrm2[at, :], m.w1[:, lanes]) + m.b1[:, lanes].astype(F32)
        square = pre * pre
        tanh = jnp.tanh(root * (pre + 0.044715 * (pre * square)))
        upper = 0.5 * (1.0 + tanh)
        m.act[at, lanes] = (pre * upper).astype(BF)
        slope = upper + 0.5 * pre * (1.0 - tanh * tanh) * (
            root * (1.0 + 3.0 * 0.044715 * square)
        )
        grad = (m.agrad[at, lanes] * slope).astype(BF)
        m.preg[at, lanes] = grad
        m.bias_sum[:, lanes] += jnp.sum(grad.astype(F32), axis=0, keepdims=True)

    nrm2_drain(three)

    def fill_nrm2(which, out, kind):
        @pl.loop(0, width // COLS)
        def _(step):
            lanes = part(step, COLS)
            out[:, lanes] = dot_nt(m.preg[part(which, group), :], m.w1[lanes, :]).astype(kind)

    finish, grad_value, grad_drain = scatter(
        fill_nrm2, m.own, m.other, m.first1, m.second1, m.relay, 9
    )

    def weight_grad(left, right, out, lanes_out):
        @pl.loop(0, width // COLS)
        def _(step):
            lanes = part(step, COLS)
            out[lanes, lanes_out] = dot_tn(left[:, lanes], right[...]).astype(BF)

    weight_grad(m.mlpg, m.act, m.grad0, slice(None))
    finish()

    def second_pull(at_row, here, there):
        upstream = grad_value(at_row)
        normed, inverse = normalise(m.middle[here, :])
        moved = norm_pull(normed, inverse, upstream * (1.0 + mod(4)))
        middle_grad = m.og[there, :].astype(F32) + moved
        m.mgrad[here, :] = middle_grad
        m.attg[there, :] = (mod(2) * middle_grad).astype(BF)
        add_sum(3, upstream)
        add_sum(4, upstream * normed)
        add_sum(2, middle_grad * m.att[here, :])

    over_share(second_pull)
    grad_drain()
    relay, finish, attg_drain = gather(m.attg, 12)
    weight_grad(m.nrm2, m.preg, m.grad1, slice(None))
    three = relay()
    finish(three)

    def fill_mlp(which, out, kind):
        @pl.loop(0, width // COLS)
        def _(step):
            lanes = part(step, COLS)
            out[:, lanes] = dot_nn(m.act[part(which, group), :], m.w2[:, lanes]).astype(kind)

    @pl.loop(0, 2)
    def _(step):
        at = part(step, group)
        m.hgrad[at, :] = dot_nt(m.attg[at, :], m.projw[...]).astype(BF)

    attg_drain(three)
    mlp_finish, mlp_value, mlp_drain = scatter(
        fill_mlp, m.own, m.other, m.first2, m.second2, m.relay, 15
    )

    @pl.loop(0, rows // TILE)
    def _(step):
        at = part(step, TILE)
        for h in range(heads):
            queries, keys = m.qkv[at, head(h, 0)], m.qkv[at, head(h, 1)]
            upstream = m.hgrad[at, h * HD : (h + 1) * HD]
            probs = m.probs[step * heads + h]
            probs_grad = dot_nt(upstream, m.qkv[at, head(h, 2)])
            value_grad = dot_tn(probs.astype(BF), upstream)
            total = jnp.sum(probs * probs_grad, axis=-1, keepdims=True)
            scores_grad = (probs * (probs_grad - total)).astype(BF)
            m.qkvg[at, head(h, 0)] = (dot_nn(scores_grad, keys) * factor).astype(BF)
            m.qkvg[at, head(h, 1)] = (dot_tn(scores_grad, queries) * factor).astype(BF)
            m.qkvg[at, head(h, 2)] = value_grad.astype(BF)

    mlp_finish()

    def block_out(at_row, here, there):
        mlp = mlp_value(at_row)
        m.out[there, :] = (m.middle[here, :] + mod(5) * mlp).astype(BF)
        add_sum(5, m.og[there, :].astype(F32) * mlp)

    over_share(block_out)
    mlp_drain()

    def fill_nrm1(which, out, kind):
        @pl.loop(0, width // COLS)
        def _(step):
            lanes = part(step, COLS)
            out[:, lanes] = dot_nt(m.qkvg[part(which, group), :], m.qkvw[lanes, :]).astype(kind)

    finish, grad1_value, grad1_drain = scatter(
        fill_nrm1, m.own, m.other, m.first3, m.second3, m.relay, 18
    )
    out_relay, out_finish, out_drain = gather(m.out, 21)
    qkv_cols = m.qkvg.shape[1]
    weight_grad(m.nrm1, m.qkvg, m.grad2, slice(0, qkv_cols))
    weight_grad(m.attg, m.heads, m.grad2, slice(qkv_cols, qkv_cols + m.heads.shape[1]))
    out_three = out_relay()
    finish()

    def first_pull(at_row, here, there):
        upstream = grad1_value(at_row)
        normed, inverse = normalise(m.tok[there, :].astype(F32))
        moved = norm_pull(normed, inverse, upstream * (1.0 + mod(1)))
        m.tokg[there, :] = (m.mgrad[here, :] + moved).astype(BF)
        add_sum(0, upstream)
        add_sum(1, upstream * normed)

    over_share(first_pull)
    grad1_drain()
    relay, finish, tokg_drain = gather(m.tokg, 24)
    out_finish(out_three)
    stores = [
        load(m.out, m.out_h, 7),
        load(m.grad0, m.grad0_h, 8),
        load(m.grad1, m.grad1_h, 9),
        load(m.grad2, m.grad2_h, 10),
        load(m.sums, m.sums_h, 11),
        load(m.bias_sum, m.bias_sum_h, 12),
    ]
    three = relay()
    finish(three)
    stores.append(load(m.tokg, m.tokg_h, 13))
    for send in sends:
        send.wait_send()
    out_drain(out_three)
    tokg_drain(three)
    for store in stores:
        store.wait()


def per_device(
    tokens,
    cond,
    seg_ids,
    ada_weight,
    ada_bias,
    qkv_weight,
    proj_weight,
    fc1_weight,
    fc1_bias,
    fc2_weight,
    out_grad,
):
    rows, width = tokens.shape
    seqs = cond.shape[0]
    share = rows // lax.axis_size("narrow")
    heads = proj_weight.shape[0] // HD
    qkv_cols, proj_rows = qkv_weight.shape[1], proj_weight.shape[0]
    hidden = fc1_weight.shape[1]
    mod_cols = ada_weight.shape[1]
    wide_index = lax.axis_index("wide")
    narrow_index = lax.axis_index("narrow")
    vmem = pltpu.VMEM
    any_spec = pl.BlockSpec(memory_space=pl.ANY)
    vmem_spec = pl.BlockSpec(memory_space=pltpu.VMEM)
    operands = (
        ("tok_h", tokens, any_spec),
        ("cond", cond, vmem_spec),
        ("seg", seg_ids, pl.BlockSpec(memory_space=pltpu.SMEM)),
        ("ada_h", ada_weight, any_spec),
        ("adab", ada_bias.reshape(1, -1), vmem_spec),
        ("qkvw_h", qkv_weight, any_spec),
        ("projw_h", proj_weight, any_spec),
        ("w1_h", fc1_weight, any_spec),
        ("b1", fc1_bias.reshape(1, -1), vmem_spec),
        ("w2_h", fc2_weight, any_spec),
        ("og_h", out_grad, any_spec),
    )
    results = (
        ("out_h", (rows, width), BF),
        ("tokg_h", (rows, width), BF),
        ("grad0_h", (width, hidden), BF),
        ("grad1_h", (width, hidden), BF),
        ("grad2_h", (width, qkv_cols + proj_rows), BF),
        ("sums_h", (8, width), F32),
        ("bias_sum_h", (1, hidden), F32),
    )
    scratch = [
        ("ada", (width, mod_cols), BF),
        ("tok", (rows, width), BF),
        ("og", (rows, width), BF),
        ("qkvw", (width, qkv_cols), BF),
        ("projw", (proj_rows, width), BF),
        ("w1", (width, hidden), BF),
        ("w2", (hidden, width), BF),
        ("mods_all", (4, seqs, mod_cols), F32),
        ("mods", (8, width), F32),
        ("sums", (8, width), F32),
        ("bias_sum", (1, hidden), F32),
        ("bias", (TILE, TILE), F32),
        ("nrm1", (rows, width), BF),
        ("qkv", (rows, qkv_cols), BF),
        ("probs", (rows // TILE * heads, TILE, TILE), F32),
        ("heads", (rows, proj_rows), BF),
        ("mlpg", (rows, width), BF),
        ("nrm2", (rows, width), BF),
        ("agrad", (rows, hidden), F32),
        ("act", (rows, hidden), BF),
        ("preg", (rows, hidden), BF),
        ("attg", (rows, width), BF),
        ("hgrad", (rows, proj_rows), BF),
        ("qkvg", (rows, qkv_cols), BF),
        ("out", (rows, width), BF),
        ("tokg", (rows, width), BF),
        ("own", (2 * share, width), F32),
        ("other", (2 * share, width), BF),
        ("relay", (share, width), BF),
        ("att", (share, width), F32),
        ("middle", (share, width), F32),
        ("mgrad", (share, width), F32),
        ("grad0", (width, hidden), BF),
        ("grad1", (width, hidden), BF),
        ("grad2", (width, qkv_cols + proj_rows), BF),
    ]
    for index in range(4):
        scratch.append((f"first{index}", (2, share, width), BF))
        scratch.append((f"second{index}", (share, width), BF))
    names = [entry[0] for entry in (*operands, *results, *scratch)] + ["loaded", "sent", "got"]
    got = pl.pallas_call(
        functools.partial(block_kernel, names, (seqs, share, width, heads)),
        out_shape=[jax.ShapeDtypeStruct(shape, kind) for _, shape, kind in results],
        in_specs=[entry[2] for entry in operands],
        out_specs=[any_spec] * len(results),
        scratch_shapes=[vmem(shape, kind) for _, shape, kind in scratch]
        + [
            pltpu.SemaphoreType.DMA((14,)),
            pltpu.SemaphoreType.DMA((27,)),
            pltpu.SemaphoreType.DMA((27,)),
        ],
        compiler_params=pltpu.CompilerParams(
            collective_id=0, has_side_effects=True, vmem_limit_bytes=67043328
        ),
        name="block",
    )(*[entry[1] for entry in operands])
    block_out, tokens_grad, grad0, grad1, grad2, sums, bias_sum = got
    cond_f = cond.astype(F32)
    silu_cond, silu_pull = jax.vjp(jax.nn.silu, cond_f)
    silu_low = silu_cond.astype(BF)
    own_seq = wide_index * rows // (P_SIZE * F)
    row = sums[:6].reshape(1, 6 * width)
    placed = jnp.where(jnp.arange(seqs)[:, None] == own_seq, row, 0.0)
    mods_all = lax.psum(placed, ("wide", "narrow"))
    mods_low = lax.dynamic_slice_in_dim(mods_all, narrow_index * mod_cols, mod_cols, 1).astype(BF)
    ada_bias_grad = jnp.sum(mods_low, axis=0, dtype=F32)
    wide_share = width // lax.axis_size("wide")
    silu_rows = lax.dynamic_slice_in_dim(silu_low, wide_index * wide_share, wide_share, 1)
    ada_weight_grad = dot_tn(silu_rows, mods_low)
    silu_grad = lax.psum(dot_nt(mods_low, ada_weight).astype(BF), "narrow").astype(F32)
    cond_grad = silu_pull(silu_grad)[0]
    fc1_bias_grad = lax.psum(bias_sum.reshape(-1), "wide")

    def spread(grad):
        full = lax.optimization_barrier(grad.astype(F32))
        return lax.psum_scatter(full, "wide", scatter_dimension=0, tiled=True)

    fc2_grad, fc1_grad, last = spread(grad0), spread(grad1), spread(grad2)
    return (
        block_out,
        tokens_grad.astype(F32),
        cond_grad,
        ada_weight_grad,
        ada_bias_grad,
        last[:, :qkv_cols],
        last[:, qkv_cols:].T,
        fc1_grad,
        fc1_bias_grad,
        fc2_grad.T,
    )


def solution(mesh):
    return jax.shard_map(
        per_device,
        mesh=mesh,
        in_specs=(
            P("wide", None),
            P(),
            P(),
            P(None, "narrow"),
            P("narrow"),
            P(None, "narrow"),
            P("narrow", None),
            P(None, "narrow"),
            P("narrow"),
            P("narrow", None),
            P("wide", None),
        ),
        out_specs=(
            P("wide", None),
            P("wide", None),
            P(),
            P("wide", "narrow"),
            P("narrow"),
            P("wide", "narrow"),
            P("narrow", "wide"),
            P("wide", "narrow"),
            P("narrow"),
            P("narrow", "wide"),
        ),
        check_vma=False,
    )
```

```python
import functools
import math

import jax
import jax.numpy as jnp
from jax import lax
from jax.experimental import pallas as pl
from jax.experimental.pallas import tpu as pltpu
from jax.sharding import PartitionSpec as P

HD = 72
F = 16
P_SIZE = 256
EPSILON = 1e-06
MASKED = -1e30
MESH = pl.DeviceIdType.MESH
BF = jnp.bfloat16
F32 = jnp.float32
TILE = 128
CHUNK = 32
COLS = 384
SUMS = 48


def dot_nn(left, right):
    return lax.dot_general(left, right, (((1,), (0,)), ((), ())), preferred_element_type=F32)


def dot_nt(left, right):
    return lax.dot_general(left, right, (((1,), (1,)), ((), ())), preferred_element_type=F32)


def dot_tn(left, right):
    return lax.dot_general(left, right, (((0,), (0,)), ((), ())), preferred_element_type=F32)


def normalise(values):
    centred = values - jnp.mean(values, axis=-1, keepdims=True)
    scale = lax.rsqrt(jnp.mean(centred * centred, axis=-1, keepdims=True) + EPSILON)
    return centred * scale, scale


def norm_pull(normed, inverse, scaled):
    mean_a = jnp.mean(scaled, axis=-1, keepdims=True)
    mean_an = jnp.mean(scaled * normed, axis=-1, keepdims=True)
    return inverse * (scaled - mean_a - normed * mean_an)


def part(index, size):
    return pl.ds(pl.multiple_of(index * size, size), size)


class Names:
    pass


def block_kernel(names, dims, *refs):
    m = Names()
    for name, ref in zip(names, refs):
        setattr(m, name, ref)
    seqs, share, width, heads, fast = dims
    rows = 4 * share
    group = 2 * share
    wide = lax.axis_index("wide")
    narrow = lax.axis_index("narrow")
    y, c = narrow // 2, narrow % 2
    seq = wide * rows // (P_SIZE * F)
    partner = (wide, y * 2 + 1 - c)
    across = (wide, (1 - y) * 2 + c)
    corner = (wide, (1 - y) * 2 + 1 - c)
    mine = 2 * c + y
    mine_y = 2 * c + 1 - y
    mine_p = 2 * (1 - c) + y
    mine_py = 2 * (1 - c) + 1 - y

    taken = [0]

    def take(count):
        taken[0] += count
        return taken[0] - count

    def remote(src, dst, index, device):
        return pltpu.make_async_remote_copy(
            src_ref=src,
            dst_ref=dst,
            send_sem=m.sent.at[index],
            recv_sem=m.got.at[index],
            device_id=device,
            device_id_type=MESH,
        )

    def load(src, dst, index):
        copy = pltpu.make_async_copy(src, dst, m.loaded.at[index])
        copy.start()
        return copy

    x, z = wide % 2, wide // 2
    flip = (z * 2 + 1 - x, narrow)
    line = [(lax.rem(z + step, 4) * 2 + x, narrow) for step in (1, 2, 3)]
    after, before = ((z + 1) * 2 + x, narrow), ((z - 1) * 2 + x, narrow)
    slab = width // 8

    barrier = pltpu.get_barrier_semaphore()
    peers = (partner, across, corner)
    greeted = (*peers, flip, *line) if fast else peers
    for peer in greeted:
        pl.semaphore_signal(barrier, inc=1, device_id=peer, device_id_type=MESH)
    half = width // 2
    proj_rows = m.projw_h.shape[0]
    thirds = [pl.ds(piece * half, half) for piece in range(m.ada.shape[0] // half)]
    get_ada = [load(m.ada_h.at[at, :], m.ada.at[at, :], 15 + k) for k, at in enumerate(thirds)]
    get_tok = load(m.tok_h, m.tok, 1)
    pl.semaphore_wait(barrier, len(greeted))

    weights = take(5)
    first_rows, last_rows = pl.ds(0, 96), pl.ds(96, proj_rows - 96)
    sends = []

    def push(src, dst, index, device):
        copy = remote(src, dst, index, device)
        copy.start()
        sends.append(copy)

    def weight_rows(owner, start=0, count=proj_rows):
        return m.projw.at[pl.ds(pl.multiple_of(owner * proj_rows + start, 16), count), :]

    cut_rows = 96
    push(m.projw_h.at[first_rows, :], weight_rows(narrow, 0, cut_rows), weights, across)

    cond = m.cond[...].astype(F32)
    low = cond * jax.nn.sigmoid(cond)
    if seqs == 1:
        low = jnp.broadcast_to(low, (16, width))
    else:
        low = jnp.concatenate([low] * (16 // seqs), axis=0)
    low = low.astype(BF)
    for piece, at in enumerate(thirds):
        lanes = slice(piece * half, (piece + 1) * half)
        get_ada[piece].wait()
        if piece == 0:
            get_qkvw = load(m.qkvw_h, m.qkvw, 2)
        m.mods_all[narrow, :, lanes] = (
            dot_nt(low, m.ada[at, :])[0:seqs] + m.adab[:, lanes].astype(F32)
        )
    moves = take(3)
    for index, peer in enumerate(peers):
        push(m.mods_all.at[narrow], m.mods_all.at[narrow], moves + index, peer)
    push(
        m.projw_h.at[last_rows, :],
        weight_rows(narrow, cut_rows, proj_rows - cut_rows),
        weights + 1,
        across,
    )
    push(m.projw_h, weight_rows(narrow), weights + 2, partner)
    get_projw = load(m.projw_h, weight_rows(narrow), 4)
    get_og = load(m.og_h, m.og, 3)
    get_w2 = load(m.w2_h, m.w2, 5)
    get_w1 = load(m.w1_h, m.w1, 6)
    get_tok.wait()

    @pl.loop(0, rows // CHUNK)
    def _(step):
        at = part(step, CHUNK)
        m.agrad[at, :], _ = normalise(m.tok[at, :].astype(F32))

    for index, peer in enumerate(peers):
        remote(m.mods_all.at[peer[1]], m.mods_all.at[peer[1]], moves + index, peer).wait_recv()
    for piece in range(12):
        m.mods[piece // 2 : piece // 2 + 1, (piece % 2) * half : (piece % 2 + 1) * half] = (
            m.mods_all[piece // 3, pl.ds(seq, 1), (piece % 3) * half : (piece % 3 + 1) * half]
        )

    def mod(index):
        return m.mods[index : index + 1, :]

    @pl.loop(0, rows // CHUNK)
    def _(step):
        at = part(step, CHUNK)
        m.nrm1[at, :] = (m.agrad[at, :] * (1.0 + mod(1)) + mod(0)).astype(BF)

    get_qkvw.wait()

    @pl.loop(0, 2)
    def _(step):
        at = part(step, group)
        m.qkv[at, :] = dot_nt(m.nrm1[at, :], m.qkvw[...]).astype(BF)

    def clip_of(axis):
        frame = lax.broadcasted_iota(jnp.int32, (TILE, TILE), axis) % F
        clip = jnp.zeros((TILE, TILE), jnp.int32)
        for spot in range(F):
            clip = jnp.where(frame == spot, m.seg[seq, spot], clip)
        return clip + 8 * (lax.broadcasted_iota(jnp.int32, (TILE, TILE), axis) // F)

    m.bias[...] = jnp.where(clip_of(0) == clip_of(1), 0.0, MASKED)
    factor = 1.0 / math.sqrt(HD)

    def head(base, which):
        start = base * 3 * HD + which * HD
        return slice(start, start + HD)

    tiles = rows // TILE
    spread = take(3 * tiles)

    def tile_of(owner, step):
        return m.heads.at[owner, part(step, TILE), :]

    @pl.loop(0, tiles)
    def _(step):
        at = part(step, TILE)
        all_scores = [
            dot_nt(m.qkv[at, head(h, 0)], m.qkv[at, head(h, 1)]) * factor + m.bias[...]
            for h in range(heads)
        ]
        all_probs = []
        for scores in all_scores:
            weight = jnp.exp(scores - jnp.max(scores, axis=-1, keepdims=True))
            all_probs.append(weight / jnp.sum(weight, axis=-1, keepdims=True))
        for h in range(heads):
            m.probs[step * heads + h] = all_probs[h]
        outs = [
            dot_nn(all_probs[h].astype(BF), m.qkv[at, head(h, 2)]).astype(BF) for h in range(heads)
        ]
        for h in range(heads):
            m.heads[narrow, at, h * HD : (h + 1) * HD] = outs[h]
        mine_tile = tile_of(narrow, step)
        remote(mine_tile, mine_tile, spread + step, across).start()
        remote(mine_tile, mine_tile, spread + tiles + step, partner).start()

    halves = 2
    piece_rows = share // halves

    def bit(base, which):
        return pl.ds(pl.multiple_of(base + which * piece_rows, CHUNK), piece_rows)

    def scatter(fill, own, other, first, second, relay):
        index = take(2 + halves)
        fill(1 - c, other, BF)
        one = remote(other.at[part(1 - y, share), :], first.at[0], index, partner)
        two = remote(other.at[part(y, share), :], first.at[1], index + 1, partner)
        one.start()
        two.start()
        fill(c, own, F32)
        one.wait_recv()
        lots = []
        for which in range(halves):
            here = bit(0, which)
            relay[here, :] = (
                own[bit((1 - y) * share, which), :] + first[0, here, :].astype(F32)
            ).astype(BF)
            lots.append(remote(relay.at[here, :], second.at[here, :], index + 2 + which, across))
            lots[-1].start()

        def finish(which):
            if which == 0:
                two.wait_recv()
            lots[which].wait_recv()

        def value(at_row):
            kept = own[pl.ds(pl.multiple_of(y * share + at_row, CHUNK), CHUNK), :]
            here = pl.ds(pl.multiple_of(at_row, CHUNK), CHUNK)
            return kept + first[1, here, :].astype(F32) + second[here, :].astype(F32)

        def drain():
            for copy in (one, two, *lots):
                copy.wait_send()

        return finish, value, drain

    def gather(buffer):
        index = take(3 * halves)
        copies = []

        def at(block, which):
            return buffer.at[bit(block * share, which), :]

        def to(block, which, place, device):
            return remote(at(block, which), at(block, which), index + place * halves + which, device)

        def begin(copy):
            copy.start()
            copies.append(copy)

        def start(which):
            begin(to(mine, which, 0, across))
            begin(to(mine, which, 1, partner))

        def relay(which):
            to(mine_y, which, 0, across).wait_recv()
            begin(to(mine_y, which, 2, partner))

        def finish():
            for which in range(halves):
                to(mine_p, which, 1, partner).wait_recv()
                to(mine_py, which, 2, partner).wait_recv()

        def drain():
            for copy in copies:
                copy.wait_send()

        return start, relay, finish, drain

    def slot_of(target):
        return jnp.where(z < 2, 3 - target, target)

    def add_rows(out, terms, count):
        @pl.loop(0, count // SUMS)
        def _(step):
            at = part(step, SUMS)
            out(at, functools.reduce(lambda a, b: a + b, [term(at).astype(F32) for term in terms]))

    def along(size, right, left, index, terms_of, source):
        def ways(step):
            return (
                (z <= step, z > 0, 3 - step + z, right, index, after),
                (3 - z <= step, z < 3, step - 3 + z, left, index + 3, before),
            )

        def hop(step):
            for active, follows, target, arrived, base, device in ways(step):

                @pl.when(active)
                def _():
                    terms = terms_of(target)
                    place = source(target)

                    def keep(at, total):
                        place[at, :] = total.astype(BF)

                    if step == 0:
                        if len(terms) > 1:
                            add_rows(keep, terms, size)
                    else:
                        last = arrived.at[step - 1]

                        @pl.when(follows)
                        def _():
                            remote(last, last, base + step - 1, device).wait_recv()
                            add_rows(keep, (*terms, lambda at: last[at, :]), size)

                        if len(terms) > 1:

                            @pl.when(jnp.logical_not(follows))
                            def _():
                                add_rows(keep, terms, size)

                    remote(place, arrived.at[step], base + step, device).start()

        def finish(out, rows_at, count):
            terms = terms_of(z)

            def ends(use, where_from):
                for arrived, base, device in where_from:
                    remote(arrived.at[2], arrived.at[2], base + 2, device).wait_recv()
                extra = [
                    (lambda at, arrived=arrived: arrived[2, rows_at(at), :])
                    for arrived, _, _ in where_from
                ]
                use([*terms, *extra])

            def total(all_terms):
                add_rows(out, all_terms, count)

            from_right, from_left = (right, index, after), (left, index + 3, before)

            @pl.when(z == 0)
            def _():
                ends(total, (from_left,))

            @pl.when(z == 3)
            def _():
                ends(total, (from_right,))

            @pl.when((z > 0) & (z < 3))
            def _():
                ends(total, (from_right, from_left))

        def drain():
            for step in range(3):
                for active, _, target, arrived, base, device in ways(step):

                    @pl.when(active)
                    def _():
                        remote(source(target), arrived.at[step], base + step, device).wait_send()

        return hop, finish, drain

    def view(grad, start, size, lanes):
        return grad.at[pl.ds(pl.multiple_of(start, 16), size), lanes]

    def flip_first(grad, lanes, landed, right, left, index, out):
        def copies(slots=range(4)):
            for slot in range(4):
                target = jnp.where(z < 2, 3 - slot, slot)
                source = view(grad, (2 * target + 1 - x) * slab, slab, lanes)
                if slot in slots:
                    yield remote(source, landed.at[slot], index + slot, flip)

        def send(slots=range(4)):
            for copy in copies(slots):
                copy.start()

        def place(target):
            return view(grad, (2 * target + x) * slab, slab, lanes)

        def terms_of(target):
            slot = slot_of(target)
            remote(landed.at[slot], landed.at[slot], index + slot, flip).wait_recv()
            spot = place(target)
            return (lambda at: spot[at, :], lambda at: landed[slot, at, :])

        hop, finish, ends = along(slab, right, left, index + 4, terms_of, place)

        def drain():
            for copy in copies():
                copy.wait_send()
            ends()

        return send, hop, lambda: finish(out, lambda at: at, slab), drain

    def line_first(grad, lanes, right, left, landed, kept, index, out):
        def place(target):
            return view(grad, 2 * target * slab, 2 * slab, lanes)

        def terms_of(target):
            spot = place(target)
            return (lambda at: spot[at, :],)

        hop, finish, ends = along(2 * slab, right, left, index, terms_of, place)
        moved = view(grad, (2 * z + 1 - x) * slab, slab, lanes)

        def settle():
            def keep(at, total):
                kept[at, :] = total

            finish(keep, lambda at: at, 2 * slab)
            there = pl.ds(pl.multiple_of((1 - x) * slab, 16), slab)

            def low(at, total):
                moved[at, :] = total.astype(BF)

            add_rows(low, (lambda at: kept.at[there, :][at, :],), slab)
            remote(moved, landed, index + 6, flip).start()

        def close():
            remote(landed, landed, index + 6, flip).wait_recv()
            here = pl.ds(pl.multiple_of(x * slab, 16), slab)
            add_rows(out, (lambda at: kept.at[here, :][at, :], lambda at: landed[at, :]), slab)

        def drain():
            remote(moved, landed, index + 6, flip).wait_send()
            ends()

        return hop, settle, close, drain

    def mine_rows(at_row):
        return pl.ds(pl.multiple_of(mine * share + at_row, CHUNK), CHUNK)

    def over_share(body, which):
        @pl.loop(0, piece_rows // CHUNK)
        def _(step):
            at_row = which * piece_rows + step * CHUNK
            body(at_row, pl.ds(pl.multiple_of(at_row, CHUNK), CHUNK), mine_rows(at_row))

    def add_sum(index, values):
        m.sums[index : index + 1, :] += jnp.sum(values, axis=0, keepdims=True)

    m.sums[...] = jnp.zeros_like(m.sums)
    qkv_cols = m.qkv.shape[1]
    if fast:
        cut = 512
        early, late = slice(0, cut), slice(cut, None)
        every = slice(None)
        final0, final1 = m.agrad.at[0:slab, :], m.agrad.at[slab : 2 * slab, :]

        def to_early(at, total):
            final0[at, early] = total

        def to_late(at, total):
            final0[at, late] = total

        def to_one(at, total):
            final1[at, :] = total

        def to_last(at, total):
            m.last_qkv[at, :] = total[:, :qkv_cols]
            m.last_proj[at, :] = total[:, qkv_cols:]

        line0_hop, line0_settle, line0_close, line0_drain = line_first(
            m.grad0, early, m.line_r, m.line_l, m.line_x, m.line_sum, take(7), to_early
        )
        send0, hop0, close0, drain0 = flip_first(
            m.grad0, late, m.land0, m.right0, m.left0, take(10), to_late
        )
        send1, hop1, close1, drain1 = flip_first(
            m.grad1, every, m.land1, m.right1, m.left1, take(10), to_one
        )
        send2, hop2, close2, drain2 = flip_first(
            m.grad2, every, m.land2, m.right2, m.left2, take(10), to_last
        )
    m.bias_sum[...] = jnp.zeros_like(m.bias_sum)

    get_og.wait()

    @pl.loop(0, rows // CHUNK)
    def _(step):
        at = part(step, CHUNK)
        m.mlpg[at, :] = (mod(5) * m.og[at, :].astype(F32)).astype(BF)

    def hidden_grad(which):
        at = part(which, group)
        m.agrad[at, :] = dot_nt(m.mlpg[at, :], m.w2[...])

    def got_weights(place, index):
        remote(place, place, index, partner).wait_recv()

    got_weights(weight_rows(across[1], 0, cut_rows), weights)
    got_weights(weight_rows(across[1], cut_rows, proj_rows - cut_rows), weights + 1)
    push(weight_rows(across[1]), weight_rows(across[1]), weights + 3, partner)
    get_w2.wait()

    def pass_on(step):
        theirs = tile_of(across[1], step)
        remote(theirs, theirs, spread + step, across).wait_recv()
        push(theirs, theirs, spread + 2 * tiles + step, partner)

    per_group = group // TILE
    for step in range(per_group):
        pass_on(step)
    hidden_grad(0)
    get_projw.wait()
    got_weights(weight_rows(partner[1]), weights + 2)
    got_weights(weight_rows(corner[1]), weights + 3)
    for which in range(2):
        if which == 1:
            for step in range(per_group, tiles):
                pass_on(step)
        for step in range(which * per_group, (which + 1) * per_group):
            for owner, index in ((partner[1], spread + tiles), (corner[1], spread + 2 * tiles)):
                theirs = tile_of(owner, step)
                remote(theirs, theirs, index + step, partner).wait_recv()

        at = pl.ds(which * group, group)

        for owner in range(4):
            lanes = slice(owner * proj_rows, (owner + 1) * proj_rows)
            m.other[:, lanes] = m.heads[owner, at, :]
        m.own[...] = dot_nn(m.other[...], m.projw[...])

        @pl.loop(0, group // CHUNK)
        def _(step):
            here = part(step, CHUNK)
            there = pl.ds(pl.multiple_of(which * group + step * CHUNK, CHUNK), CHUNK)
            middle = m.tok[there, :].astype(F32) + mod(2) * m.own[here, :]
            normed, _ = normalise(middle)
            m.nrm2[there, :] = (normed * (1.0 + mod(4)) + mod(3)).astype(BF)

        @pl.when(c == which)
        def _():
            att = m.own[part(y, share), :]
            m.att[...] = att
            m.middle[...] = m.tok[part(mine, share), :].astype(F32) + mod(2) * att

    hidden_grad(1)
    get_w1.wait()
    root = math.sqrt(2.0 / math.pi)

    @pl.loop(0, 2 * (m.w1.shape[1] // COLS))
    def _(step):
        at = part(step % 2, group)
        lanes = part(step // 2, COLS)
        pre = dot_nn(m.nrm2[at, :], m.w1[:, lanes]) + m.b1[:, lanes].astype(F32)
        square = pre * pre
        tanh = jnp.tanh(root * (pre + 0.044715 * (pre * square)))
        upper = 0.5 * (1.0 + tanh)
        m.act[at, lanes] = (pre * upper).astype(BF)
        slope = upper + 0.5 * pre * (1.0 - tanh * tanh) * (
            root * (1.0 + 3.0 * 0.044715 * square)
        )
        grad = (m.agrad[at, lanes] * slope).astype(BF)
        m.preg[at, lanes] = grad
        m.bias_sum[:, lanes] += jnp.sum(grad.astype(F32), axis=0, keepdims=True)

    def weight_grad(left, right, out, lanes_out):
        out[:, lanes_out] = dot_tn(left[...], right[...]).astype(BF)

    weight_grad(m.mlpg, m.act, m.grad0, slice(None))
    if fast:
        send0()
        line0_hop(0)

    def fill_nrm2(which, out, kind):
        out[...] = dot_nt(m.preg[part(which, group), :], m.w1[...]).astype(kind)

    finish, grad_value, grad_drain = scatter(
        fill_nrm2, m.own, m.other, m.first1, m.second1, m.relay
    )

    weight_grad(m.nrm2, m.preg, m.grad1, slice(None))
    if fast:
        send1()
        line0_hop(1)
        hop0(0)

    def second_pull(at_row, here, there):
        upstream = grad_value(at_row)
        normed, inverse = normalise(m.middle[here, :])
        moved = norm_pull(normed, inverse, upstream * (1.0 + mod(4)))
        middle_grad = m.og[there, :].astype(F32) + moved
        m.mgrad[here, :] = middle_grad
        m.attg[there, :] = (mod(2) * middle_grad).astype(BF)
        add_sum(3, upstream)
        add_sum(4, upstream * normed)
        add_sum(2, middle_grad * m.att[here, :])

    start, relay, attg_finish, attg_drain = gather(m.attg)
    for which in range(halves):
        finish(which)
        over_share(second_pull, which)
        start(which)
    grad_drain()

    def fill_mlp(which, out, kind):
        out[...] = dot_nn(m.act[part(which, group), :], m.w2[...]).astype(kind)

    mlp_finish, mlp_value, mlp_drain = scatter(
        fill_mlp, m.own, m.other, m.first2, m.second2, m.relay
    )
    for which in range(halves):
        relay(which)
    if fast:
        line0_hop(2)
    attg_finish()

    @pl.loop(0, 2)
    def _(step):
        at = part(step, group)
        m.hgrad[at, :] = dot_nt(m.attg[at, :], weight_rows(narrow)[...]).astype(BF)


    def attention_pull(step):
        at = part(step, TILE)
        every_head = range(heads)
        queries = [m.qkv[at, head(h, 0)] for h in every_head]
        keys = [m.qkv[at, head(h, 1)] for h in every_head]
        upstream = [m.hgrad[at, h * HD : (h + 1) * HD] for h in every_head]
        probs_grad = [dot_nt(upstream[h], m.qkv[at, head(h, 2)]) for h in every_head]
        value_grad = [
            dot_tn(m.probs[step * heads + h].astype(BF), upstream[h]) for h in every_head
        ]
        scores_grad = []
        for h in every_head:
            probs = m.probs[step * heads + h]
            total = jnp.sum(probs * probs_grad[h], axis=-1, keepdims=True)
            scores_grad.append((probs * (probs_grad[h] - total)).astype(BF))
        query_grad = [dot_nn(scores_grad[h], keys[h]) * factor for h in every_head]
        key_grad = [dot_tn(scores_grad[h], queries[h]) * factor for h in every_head]
        for h in every_head:
            m.qkvg[at, head(h, 0)] = query_grad[h].astype(BF)
            m.qkvg[at, head(h, 1)] = key_grad[h].astype(BF)
            m.qkvg[at, head(h, 2)] = value_grad[h].astype(BF)

    def block_out(at_row, here, there):
        mlp = mlp_value(at_row)
        m.out[there, :] = (m.middle[here, :] + mod(5) * mlp).astype(BF)
        add_sum(5, m.og[there, :].astype(F32) * mlp)

    out_start, out_relay, out_finish, out_drain = gather(m.out)

    pl.loop(0, tiles // 2)(attention_pull)
    if fast:
        hop0(1)
    for which in range(halves):
        mlp_finish(which)
        over_share(block_out, which)
        out_start(which)
    mlp_drain()
    if fast:
        hop1(0)
    pl.loop(tiles // 2, tiles)(attention_pull)
    if fast:
        hop0(2)
    weight_grad(m.nrm1, m.qkvg, m.grad2, slice(0, qkv_cols))
    weight_grad(m.attg, m.heads.at[narrow], m.grad2, slice(qkv_cols, None))
    if fast:
        send2((0,))

    def fill_nrm1(which, out, kind):
        out[...] = dot_nn(m.qkvg[part(which, group), :], m.qkvw[...]).astype(kind)

    finish, grad1_value, grad1_drain = scatter(
        fill_nrm1, m.own, m.other, m.first3, m.second3, m.relay
    )
    for which in range(halves):
        out_relay(which)
    if fast:
        hop1(1)

    def first_pull(at_row, here, there):
        upstream = grad1_value(at_row)
        normed, inverse = normalise(m.tok[there, :].astype(F32))
        moved = norm_pull(normed, inverse, upstream * (1.0 + mod(1)))
        m.tokg[there, :] = (m.mgrad[here, :] + moved).astype(BF)
        add_sum(0, upstream)
        add_sum(1, upstream * normed)

    start, relay, tokg_finish, tokg_drain = gather(m.tokg)
    for which in range(halves):
        finish(which)
        over_share(first_pull, which)
        start(which)
    grad1_drain()
    out_finish()
    def heads_drain():
        for step in range(tiles):
            mine_tile = tile_of(narrow, step)
            remote(mine_tile, mine_tile, spread + step, across).wait_send()
            remote(mine_tile, mine_tile, spread + tiles + step, partner).wait_send()

    if not fast:
        stores = [
            load(m.out, m.out_h, 7),
            load(m.grad0, m.grad0_h, 8),
            load(m.grad1, m.grad1_h, 9),
            load(m.grad2, m.grad2_h, 10),
            load(m.sums, m.sums_h, 11),
            load(m.bias_sum, m.bias_sum_h, 12),
        ]
        for which in range(halves):
            relay(which)
        tokg_finish()
        stores.append(load(m.tokg, m.tokg_h, 13))
        for send in sends:
            send.wait_send()
        for drain in (heads_drain, attg_drain, out_drain, tokg_drain):
            drain()
        for store in stores:
            store.wait()
        return

    stores = [load(m.out, m.out_h, 7)]
    mod_cols = m.mods_all.shape[2]
    padded = m.vector.shape[1] - m.bias_sum.shape[1]
    for piece in range(12):
        m.pieces[piece // 3, :, (piece % 3) * half : (piece % 3 + 1) * half] = (
            m.sums[piece // 2 : piece // 2 + 1, (piece % 2) * half : (piece % 2 + 1) * half]
        )
    m.parts[narrow] = m.pieces[narrow]
    summed, flat, lined, conds = take(3), take(1), take(3), take(3)
    for index, peer in enumerate(peers):
        push(m.pieces.at[peer[1]], m.parts.at[narrow], summed + index, peer)
    for which in range(halves):
        relay(which)
    for index, peer in enumerate(peers):
        remote(m.parts.at[peer[1]], m.parts.at[peer[1]], summed + index, peer).wait_recv()
    m.vector[...] = jnp.zeros_like(m.vector)
    m.vector[:, :mod_cols] = (m.parts[0] + m.parts[1]) + (m.parts[2] + m.parts[3])
    m.vector[:, padded:] = m.bias_sum[...]
    push(m.vector, m.flipped, flat, flip)
    send2((1, 2, 3))
    line0_settle()
    hop1(2)
    tokg_finish()
    stores.append(load(m.tokg, m.tokg_h, 8))
    remote(m.flipped, m.flipped, flat, flip).wait_recv()
    m.lined[z] = m.vector[...] + m.flipped[...]
    for index, peer in enumerate(line):
        push(m.lined.at[z], m.lined.at[z], lined + index, peer)
    hop2(0)
    close0()
    for index in range(3):
        source = lax.rem(z + 3 - index, 4)
        remote(m.lined.at[source], m.lined.at[source], lined + index, line[index]).wait_recv()
    total = (m.lined[0] + m.lined[1]) + (m.lined[2] + m.lined[3])
    m.vector_out[...] = total
    low_rows = jnp.broadcast_to(total[:, :mod_cols], (16, mod_cols)).astype(BF)
    m.conds[narrow] = dot_nn(low_rows, m.ada[...])[0:1]
    stores.append(load(m.vector_out, m.vector_h, 9))
    for index, peer in enumerate(peers):
        push(m.conds.at[narrow], m.conds.at[narrow], conds + index, peer)
    hop2(1)
    close1()
    stores.append(load(final1, m.grad1_h, 12))
    for index, peer in enumerate(peers):
        remote(m.conds.at[peer[1]], m.conds.at[peer[1]], conds + index, peer).wait_recv()
    m.cond_out[...] = (m.conds[0] + m.conds[1]) + (m.conds[2] + m.conds[3])
    stores.append(load(m.cond_out, m.cond_h, 11))
    hop2(2)
    line0_close()
    stores.append(load(final0, m.grad0_h, 10))
    close2()
    stores.append(load(m.last_qkv, m.last_qkv_h, 13))
    stores.append(load(m.last_proj, m.last_proj_h, 14))
    for send in sends:
        send.wait_send()
    for drain in (heads_drain, attg_drain, out_drain, tokg_drain):
        drain()
    for drain in (line0_drain, drain0, drain1, drain2):
        drain()
    for store in stores:
        store.wait()


def per_device(
    tokens,
    cond,
    seg_ids,
    ada_weight,
    ada_bias,
    qkv_weight,
    proj_weight,
    fc1_weight,
    fc1_bias,
    fc2_weight,
    out_grad,
):
    rows, width = tokens.shape
    seqs = cond.shape[0]
    share = rows // lax.axis_size("narrow")
    heads = proj_weight.shape[0] // HD
    qkv_cols, proj_rows = qkv_weight.shape[1], proj_weight.shape[0]
    hidden = fc1_weight.shape[1]
    mod_cols = ada_weight.shape[1]
    wide_index = lax.axis_index("wide")
    narrow_index = lax.axis_index("narrow")
    vmem = pltpu.VMEM
    any_spec = pl.BlockSpec(memory_space=pl.ANY)
    vmem_spec = pl.BlockSpec(memory_space=pltpu.VMEM)
    operands = (
        ("tok_h", tokens, any_spec),
        ("cond", cond, vmem_spec),
        ("seg", seg_ids, pl.BlockSpec(memory_space=pltpu.SMEM)),
        ("ada_h", ada_weight.T, any_spec),
        ("adab", ada_bias.reshape(1, -1), vmem_spec),
        ("qkvw_h", qkv_weight.T, any_spec),
        ("projw_h", proj_weight, any_spec),
        ("w1_h", fc1_weight, any_spec),
        ("b1", fc1_bias.reshape(1, -1), vmem_spec),
        ("w2_h", fc2_weight, any_spec),
        ("og_h", out_grad, any_spec),
    )
    fast = lax.axis_size("wide") == 8 and seqs == 1
    slab = width // 8
    padded = (mod_cols + 127) // 128 * 128 + hidden
    results = (
        ("out_h", (rows, width), BF),
        ("tokg_h", (rows, width), BF),
        ("grad0_h", (slab, hidden), F32),
        ("grad1_h", (slab, hidden), F32),
        ("last_qkv_h", (slab, qkv_cols), F32),
        ("last_proj_h", (slab, proj_rows), F32),
        ("vector_h", (1, padded), F32),
        ("cond_h", (1, width), F32),
    ) if fast else (
        ("out_h", (rows, width), BF),
        ("tokg_h", (rows, width), BF),
        ("grad0_h", (width, hidden), BF),
        ("grad1_h", (width, hidden), BF),
        ("grad2_h", (width, qkv_cols + proj_rows), BF),
        ("sums_h", (8, width), F32),
        ("bias_sum_h", (1, hidden), F32),
    )
    scratch = [
        ("ada", (mod_cols, width), BF),
        ("tok", (rows, width), BF),
        ("og", (rows, width), BF),
        ("qkvw", (qkv_cols, width), BF),
        ("projw", (4 * proj_rows, width), BF),
        ("w1", (width, hidden), BF),
        ("w2", (hidden, width), BF),
        ("mods_all", (4, seqs, mod_cols), F32),
        ("mods", (8, width), F32),
        ("sums", (8, width), F32),
        ("bias_sum", (1, hidden), F32),
        ("bias", (TILE, TILE), F32),
        ("nrm1", (rows, width), BF),
        ("qkv", (rows, qkv_cols), BF),
        ("probs", (rows // TILE * heads, TILE, TILE), F32),
        ("heads", (4, rows, proj_rows), BF),
        ("mlpg", (rows, width), BF),
        ("nrm2", (rows, width), BF),
        ("agrad", (rows, hidden), F32),
        ("act", (rows, hidden), BF),
        ("preg", (rows, hidden), BF),
        ("attg", (rows, width), BF),
        ("hgrad", (rows, proj_rows), BF),
        ("qkvg", (rows, qkv_cols), BF),
        ("out", (rows, width), BF),
        ("tokg", (rows, width), BF),
        ("own", (2 * share, width), F32),
        ("other", (2 * share, width), BF),
        ("relay", (share, width), BF),
        ("att", (share, width), F32),
        ("middle", (share, width), F32),
        ("mgrad", (share, width), F32),
        ("grad0", (width, hidden), BF),
        ("grad1", (width, hidden), BF),
        ("grad2", (width, qkv_cols + proj_rows), BF),
    ]
    for index in range(1, 4):
        scratch.append((f"first{index}", (2, share, width), BF))
        scratch.append((f"second{index}", (share, width), BF))
    if fast:
        cut = 512
        scratch += [
            ("line_r", (3, 2 * slab, cut), BF),
            ("line_l", (3, 2 * slab, cut), BF),
            ("line_x", (slab, cut), BF),
            ("line_sum", (2 * slab, cut), F32),
            ("last_qkv", (slab, qkv_cols), F32),
            ("last_proj", (slab, proj_rows), F32),
            ("pieces", (4, 1, mod_cols), F32),
            ("parts", (4, 1, mod_cols), F32),
            ("vector", (1, padded), F32),
            ("flipped", (1, padded), F32),
            ("lined", (4, 1, padded), F32),
            ("vector_out", (1, padded), F32),
            ("conds", (4, 1, width), F32),
            ("cond_out", (1, width), F32),
        ]
        for index, cols in enumerate((hidden - cut, hidden, qkv_cols + proj_rows)):
            scratch.append((f"land{index}", (4, slab, cols), BF))
            scratch.append((f"right{index}", (3, slab, cols), BF))
            scratch.append((f"left{index}", (3, slab, cols), BF))
    names = [entry[0] for entry in (*operands, *results, *scratch)] + ["loaded", "sent", "got"]
    got = pl.pallas_call(
        functools.partial(block_kernel, names, (seqs, share, width, heads, fast)),
        out_shape=[jax.ShapeDtypeStruct(shape, kind) for _, shape, kind in results],
        in_specs=[entry[2] for entry in operands],
        out_specs=[any_spec] * len(results),
        scratch_shapes=[vmem(shape, kind) for _, shape, kind in scratch]
        + [
            pltpu.SemaphoreType.DMA((18,)),
            pltpu.SemaphoreType.DMA((100,)),
            pltpu.SemaphoreType.DMA((100,)),
        ],
        compiler_params=pltpu.CompilerParams(
            collective_id=0, has_side_effects=True, vmem_limit_bytes=67043328
        ),
        name="block",
    )(*[entry[1] for entry in operands])
    cond_f = cond.astype(F32)
    silu_cond, silu_pull = jax.vjp(jax.nn.silu, cond_f)
    silu_low = silu_cond.astype(BF)
    if fast:
        block_out, tokens_grad, fc2_grad, fc1_grad, qkv_grad, proj_grad, vector, cond_sum = got
        mods_low = vector[:, :mod_cols].astype(BF)
        silu_rows = lax.dynamic_slice_in_dim(silu_low, wide_index * slab, slab, 1)
        return (
            block_out,
            tokens_grad.astype(F32),
            silu_pull(cond_sum)[0],
            silu_rows.astype(F32).T * mods_low.astype(F32),
            mods_low[0].astype(F32),
            qkv_grad,
            proj_grad.T,
            fc1_grad,
            vector[0, padded - hidden :],
            fc2_grad.T,
        )
    block_out, tokens_grad, grad0, grad1, grad2, sums, bias_sum = got
    own_seq = wide_index * rows // (P_SIZE * F)
    row = sums[:6].reshape(1, 6 * width)
    placed = jnp.where(jnp.arange(seqs)[:, None] == own_seq, row, 0.0)
    mods_all = lax.psum(placed, ("wide", "narrow"))
    mods_low = lax.dynamic_slice_in_dim(mods_all, narrow_index * mod_cols, mod_cols, 1).astype(BF)
    ada_bias_grad = jnp.sum(mods_low, axis=0, dtype=F32)
    wide_share = width // lax.axis_size("wide")
    silu_rows = lax.dynamic_slice_in_dim(silu_low, wide_index * wide_share, wide_share, 1)
    ada_weight_grad = dot_tn(silu_rows, mods_low)
    silu_grad = lax.psum(dot_nt(mods_low, ada_weight).astype(BF), "narrow").astype(F32)
    cond_grad = silu_pull(silu_grad)[0]
    fc1_bias_grad = lax.psum(bias_sum.reshape(-1), "wide")

    def spread(grad):
        full = lax.optimization_barrier(grad.astype(F32))
        return lax.psum_scatter(full, "wide", scatter_dimension=0, tiled=True)

    fc2_grad, fc1_grad, last = spread(grad0), spread(grad1), spread(grad2)
    return (
        block_out,
        tokens_grad.astype(F32),
        cond_grad,
        ada_weight_grad,
        ada_bias_grad,
        last[:, :qkv_cols],
        last[:, qkv_cols:].T,
        fc1_grad,
        fc1_bias_grad,
        fc2_grad.T,
    )


def solution(mesh):
    return jax.shard_map(
        per_device,
        mesh=mesh,
        in_specs=(
            P("wide", None),
            P(),
            P(),
            P(None, "narrow"),
            P("narrow"),
            P(None, "narrow"),
            P("narrow", None),
            P(None, "narrow"),
            P("narrow"),
            P("narrow", None),
            P("wide", None),
        ),
        out_specs=(
            P("wide", None),
            P("wide", None),
            P(),
            P("wide", "narrow"),
            P("narrow"),
            P("wide", "narrow"),
            P("narrow", "wide"),
            P("wide", "narrow"),
            P("narrow"),
            P("narrow", "wide"),
        ),
        check_vma=False,
    )
```
